512 devices in a mesh: orb: 32 (over y, z_hi, core), aux: 16 (over x, z_lo).
Axes of the slice: x: 4, y: 8, z: 8 (z_hi: 2, z_lo: 4; z = z_hi * 4 + z_lo), core: 2. Of those that a mesh axis runs over, the one named last changes fastest.
Arguments:
- orbital_slabs: float32 [32, 8192, 1024], P('orb', 'aux'), may hold values from -0.625 to 0.625
- occupied_energy: float32 [32], replicated, may hold values from -1.5 to -0.3
- virtual_energy: float32 [1024], replicated, may hold values from 0.3 to 2.5
- virtual_count: int32 [32], replicated, may hold values from 512 to 1024, as said below
Outputs:
- density: float32 [32, 8192, 1024], P('orb', 'aux')
The draws below stay inside these ranges and needn't reach their ends.
Inputs may be any that keep to these rules, and one draw needn't show every extreme that they name: `virtual_count`: the largest count is 1024 in every draw.
All inputs are finite; a program needn't handle non-finite values.
Results may differ from the reference program's by a relative error of at most 0.0003.
Values sent between devices are 32-bit elements; how exact they have to be, the bound alone decides.
No kernel may reach another device: no remote copies, remote signals or barrier semaphores. Data moves between devices by JAX's collectives and lax.ppermute only.
A program may use at most 64 MiB of HBM per device.

```python
import jax
import jax.numpy as jnp
from jax import lax

NV = 1024
NAUX = 8192
ROUNDS = 1
NOCC = 32


def draw_virtual_count(key, part):
    key_counts, key_pick = jax.random.split(key)
    counts = jax.random.randint(key_counts, (NOCC,), NV // 2, NV + 1)
    picked = jax.random.randint(key_pick, (), 0, NOCC)
    return jnp.where(jnp.arange(NOCC) == picked, NV, counts).astype(jnp.int32)


def block_levels(key, shape, pieces, least, top_value):
    level = 1.0
    for dim, shards_of in pieces:
        draws = jax.random.uniform(jax.random.fold_in(jax.random.fold_in(key, 6), dim), (shards_of,), jnp.float32, least / len(pieces), top_value / len(pieces))
        level = level * jnp.repeat(jnp.exp(draws), shape[dim] // shards_of).reshape((-1,) + (1,) * (len(shape) - 1 - dim))
    return level


def bell_draw(rng, dims, spread, reach, cuts=(), kind=jnp.bfloat16):
    values = jax.random.normal(rng, dims, jnp.float32) * spread
    if len(cuts) > 0:
        values = block_levels(rng, dims, cuts, -0.22, 0.18) * values
    return jnp.clip(values, min=-reach, max=reach).astype(kind)


def setup_inputs(seed: int = 0) -> dict:
    streams_of = jax.random.split(jax.random.key(seed), 5)
    return {
        "orbital_slabs": bell_draw(streams_of[0], (NOCC, NAUX, NV), (NAUX ** 0.5) ** -0.5, 0.625, ((0, 32), (1, 16)), jnp.float32),
        "occupied_energy": jnp.clip(jax.random.uniform(streams_of[1], (NOCC,), jnp.float32, -1.5, -0.3), -1.5, -0.3),
        "virtual_energy": jnp.clip(jax.random.uniform(streams_of[2], (NV,), jnp.float32, 0.3, 2.5), 0.3, 2.5),
        "virtual_count": draw_virtual_count(jax.random.fold_in(streams_of[4], 71), 0),
    }


highest_mode = lax.Precision.HIGHEST


def amplitudes(coupling, occupied_energy, virtual_energy, virtual_count, orbital_one, orbital_two):
    positions = jnp.arange(virtual_energy.shape[0], dtype=jnp.int32)
    mask_one = (positions < virtual_count[orbital_one]).astype(jnp.float32)
    mask_two = (positions < virtual_count[orbital_two]).astype(jnp.float32)
    denominator = virtual_energy[:, None] + virtual_energy[None, :] - occupied_energy[orbital_one] - occupied_energy[orbital_two]
    return (2.0 * coupling - coupling.T) * mask_one[:, None] * mask_two[None, :] / denominator


def reference(orbital_slabs, occupied_energy, virtual_energy, virtual_count):
    orbitals = orbital_slabs.shape[0]
    density = jnp.zeros(orbital_slabs.shape, jnp.float32)
    for distance in range(1, ROUNDS + 1):
        def advance(density, orbital_one):
            orbital_two = ((orbital_one + distance) % orbitals).astype(jnp.int32)
            slab_one = lax.dynamic_index_in_dim(orbital_slabs, orbital_one, 0, keepdims=False)
            slab_two = lax.dynamic_index_in_dim(orbital_slabs, orbital_two, 0, keepdims=False)
            coupling = lax.dot_general(slab_one, slab_two, (((0,), (0,)), ((), ())), precision=highest_mode, preferred_element_type=jnp.float32)
            amplitude = amplitudes(coupling, occupied_energy, virtual_energy, virtual_count, orbital_one, orbital_two)
            term_one = lax.dot_general(slab_two, amplitude, (((1,), (1,)), ((), ())), precision=highest_mode, preferred_element_type=jnp.float32)
            term_two = jnp.dot(slab_one, amplitude, precision=highest_mode, preferred_element_type=jnp.float32)
            density = density.at[orbital_one].add(term_one)
            density = density.at[orbital_two].add(term_two)
            return density, None

        density, unused = lax.scan(advance, density, jnp.arange(orbitals, dtype=jnp.int32))
    return density
```

```python
import jax
import jax.numpy as jnp
from jax import lax
from jax.sharding import PartitionSpec as P


ORB, AUX = 32, 16
AXES = ("orb", "aux")
X, ZL = 4, 4
QUARTER, HALF_Q, COLS = 256, 128, 512
ROWS = 256


def route(step):
    pairs = []
    for orbital in range(ORB):
        for shard in range(AUX):
            target = step(orbital, shard // ZL, shard % ZL)
            if target is not None:
                o, x, z = target
                pairs.append((orbital * AUX + shard, o % ORB * AUX + x % X * ZL + z))
    return pairs


SWAP = route(lambda o, x, z: (o ^ 1, x, z))
DOWN = [route(lambda o, x, z: (o - 2 + c, x, z) if o % 2 == 0 else None) for c in (0, 1)]
UP = [route(lambda o, x, z: (o + 2 - c, x, z) if o % 2 == c else None) for c in (0, 1)]
AROUND = [route(lambda o, x, z: (o, x + r, z)) for r in range(X)]
ALONG = [route(lambda o, x, z: (o, x, z ^ d)) for d in range(ZL)]


def move(block, pairs):
    return lax.ppermute(block, AXES, pairs)


def dot(a, b, da, db):
    return lax.dot_general(
        a,
        b,
        (((da,), (db,)), ((), ())),
        precision=lax.Precision.HIGH,
        preferred_element_type=jnp.float32,
    )


def rows_at(block, start, size):
    return lax.dynamic_slice_in_dim(block, start, size, 0)


def cols_at(block, start, size):
    return lax.dynamic_slice_in_dim(block, start, size, 1)


def after(value, *earlier):
    return lax.optimization_barrier((value, earlier))[0]


def pair_term(one, two, two_cols, one_cols):
    return 2.0 * dot(one, two_cols, 0, 0) - dot(two, one_cols, 0, 0)


def shards(orbital_slabs, occupied_energy, virtual_energy, virtual_count):
    own = orbital_slabs[0]
    orbital = lax.axis_index("orb")
    shard = lax.axis_index("aux")
    core, base = orbital % 2, orbital - orbital % 2
    px, pz = shard // ZL, shard % ZL
    bit = pz % 2
    first = core == 0
    at = core * COLS

    def send_x(term):
        return [rows_at(term, (px + r) % X * QUARTER, QUARTER) for r in range(X)]

    def add_x(parts):
        return (parts[0] + parts[1]) + (parts[2] + parts[3])

    def around(parts):
        return [parts[0]] + [move(parts[r], AROUND[r]) for r in (1, 2, 3)]

    def halves(total):
        return rows_at(total, bit * HALF_Q, HALF_Q), rows_at(
            total, (1 - bit) * HALF_Q, HALF_Q
        )

    def amplitude(term, left, right, col):
        row = px * QUARTER + bit * HALF_Q
        rows = row + jnp.arange(term.shape[0], dtype=jnp.int32)
        cols = col + jnp.arange(term.shape[1], dtype=jnp.int32)
        energy_rows = lax.dynamic_slice_in_dim(virtual_energy, row, term.shape[0])
        energy_cols = lax.dynamic_slice_in_dim(virtual_energy, col, term.shape[1])
        keep_rows = (rows < virtual_count[left]).astype(jnp.float32)
        keep_cols = (cols < virtual_count[right]).astype(jnp.float32)
        denominator = (
            energy_rows[:, None]
            + energy_cols[None, :]
            - occupied_energy[left]
            - occupied_energy[right]
        )
        return term * keep_rows[:, None] * keep_cols[None, :] / denominator

    def join(part, other):
        return jnp.where(
            bit == 0,
            jnp.concatenate([part, other], 0),
            jnp.concatenate([other, part], 0),
        )

    def in_order(pieces):
        whole = jnp.zeros((X * QUARTER, pieces[0].shape[1]), jnp.float32)
        for r, piece in enumerate(pieces):
            whole = lax.dynamic_update_slice_in_dim(
                whole, piece, (px - r) % X * QUARTER, 0
            )
        return whole

    one, two, three = base, base + 1, (base + 2) % ORB

    arrived = [move(own[c * ROWS : (c + 1) * ROWS], DOWN[c]) for c in (0, 1)]
    other = move(own, SWAP)
    slab_one = jnp.where(first, own, other)
    slab_two = jnp.where(first, other, own)
    one_cols = cols_at(slab_one, at, COLS)
    two_cols = cols_at(slab_two, at, COLS)

    inner_sends = send_x(pair_term(slab_one, slab_two, two_cols, one_cols))
    inner_parts = around(inner_sends)
    inner_kept, inner_sent = halves(add_x(inner_parts))
    inner_kept_next = inner_kept + move(inner_sent, ALONG[1])

    near_two = rows_at(slab_two, core * ROWS, ROWS)
    far_two = rows_at(slab_two, (1 - core) * ROWS, ROWS)
    near_two_cols, far_two_cols = cols_at(near_two, at, COLS), cols_at(far_two, at, COLS)
    arrived = after(arrived, inner_sent, near_two, far_two, near_two_cols, far_two_cols)
    near = jnp.where(first, arrived[0], arrived[1])
    far = move(near, SWAP)
    near_cols = cols_at(near, at, COLS)
    outer_near = pair_term(near_two, near, near_cols, near_two_cols)
    far = after(far, outer_near)
    far_cols = cols_at(far, at, COLS)
    outer = outer_near + pair_term(far_two, far, far_cols, far_two_cols)
    outer_sends = send_x(outer)
    outer_parts = around(outer_sends)

    inner_kept = after(inner_kept_next, outer_sends)
    inner_kept = inner_kept + move(inner_kept, ALONG[2])
    inner_t = amplitude(inner_kept, one, two, at)
    inner_other = move(inner_t, ALONG[1])

    outer_kept, outer_sent = halves(add_x(after(outer_parts, inner_t)))
    outer_other = move(outer_sent, ALONG[1])
    inner_quarter = join(inner_t, after(inner_other, outer_sent))
    inner_pieces = around([inner_quarter] * X)
    outer_kept = outer_kept + after(outer_other, inner_quarter)
    outer_kept = outer_kept + move(outer_kept, ALONG[2])
    outer_t = amplitude(outer_kept, two, three, at)
    outer_quarter = join(outer_t, move(outer_t, ALONG[1]))
    outer_pieces = around([outer_quarter] * X)

    inner_all = in_order(after(inner_pieces, outer_quarter))
    to_one = dot(two_cols, inner_all, 1, 1)
    to_two = dot(slab_one, inner_all, 1, 0)

    outer_all = in_order(after(outer_pieces, to_one, to_two))
    outgoing = dot(slab_two, outer_all, 1, 0)
    incoming = [move(outgoing, UP[c]) for c in (0, 1)]

    three_cols = jnp.where(
        first,
        jnp.concatenate([near_cols, far_cols], 0),
        jnp.concatenate([far_cols, near_cols], 0),
    )
    beyond = dot(three_cols, after(outer_all, outgoing), 1, 1)
    blank = jnp.zeros_like(to_two)
    to_two = beyond + jnp.where(
        first,
        jnp.concatenate([to_two, blank], 1),
        jnp.concatenate([blank, to_two], 1),
    )
    crossed = move(jnp.where(first, to_two, to_one), SWAP)
    density = jnp.where(first, to_one, to_two) + crossed
    density = density + jnp.concatenate(after(incoming, density), 1)
    return density[None]


def solution(mesh):
    placed = (P("orb", "aux", None), P(), P(), P())
    return jax.shard_map(
        shards, mesh=mesh, in_specs=placed, out_specs=P("orb", "aux", None), check_vma=False
    )
```

```python
import jax
import jax.numpy as jnp
from jax import lax
from jax.sharding import PartitionSpec as P


ORB, AUX = 32, 16
AXES = ("orb", "aux")
X, ZL = 4, 4
QUARTER, HALF_Q, COLS = 256, 128, 512
ROWS, CHUNK = 256, 256


def route(step):
    pairs = []
    for orbital in range(ORB):
        for shard in range(AUX):
            target = step(orbital, shard // ZL, shard % ZL)
            if target is not None:
                o, x, z = target
                pairs.append((orbital * AUX + shard, o % ORB * AUX + x % X * ZL + z))
    return pairs


SWAP = route(lambda o, x, z: (o ^ 1, x, z))
DOWN = [route(lambda o, x, z: (o - 2 + c, x, z) if o % 2 == 0 else None) for c in (0, 1)]
UP = [route(lambda o, x, z: (o + 2 - c, x, z) if o % 2 == c else None) for c in (0, 1)]
AROUND = [route(lambda o, x, z: (o, x + r, z)) for r in range(X)]
ALONG = [route(lambda o, x, z: (o, x, z ^ d)) for d in range(ZL)]


def move(block, pairs):
    return lax.ppermute(block, AXES, pairs)


def dot(a, b, da, db):
    return lax.dot_general(
        a,
        b,
        (((da,), (db,)), ((), ())),
        precision=lax.Precision.HIGH,
        preferred_element_type=jnp.float32,
    )


def rows_at(block, start, size):
    return lax.dynamic_slice_in_dim(block, start, size, 0)


def cols_at(block, start, size):
    return lax.dynamic_slice_in_dim(block, start, size, 1)


def after(value, *earlier):
    return lax.optimization_barrier((value, earlier))[0]


def pair_term(one, two, two_cols, one_cols):
    return 2.0 * dot(one, two_cols, 0, 0) - dot(two, one_cols, 0, 0)


def shards(orbital_slabs, occupied_energy, virtual_energy, virtual_count):
    own = orbital_slabs[0]
    orbital = lax.axis_index("orb")
    shard = lax.axis_index("aux")
    core, base = orbital % 2, orbital - orbital % 2
    px, pz = shard // ZL, shard % ZL
    bit = pz % 2
    first = core == 0
    at = core * COLS

    def send_x(term):
        return [rows_at(term, (px + r) % X * QUARTER, QUARTER) for r in range(X)]

    def add_x(parts):
        return (parts[0] + parts[1]) + (parts[2] + parts[3])

    def around(parts):
        return [parts[0]] + [move(parts[r], AROUND[r]) for r in (1, 2, 3)]

    def halves(total):
        return rows_at(total, bit * HALF_Q, HALF_Q), rows_at(
            total, (1 - bit) * HALF_Q, HALF_Q
        )

    def amplitude(term, left, right, col):
        row = px * QUARTER + bit * HALF_Q
        rows = row + jnp.arange(term.shape[0], dtype=jnp.int32)
        cols = col + jnp.arange(term.shape[1], dtype=jnp.int32)
        energy_rows = lax.dynamic_slice_in_dim(virtual_energy, row, term.shape[0])
        energy_cols = lax.dynamic_slice_in_dim(virtual_energy, col, term.shape[1])
        keep_rows = (rows < virtual_count[left]).astype(jnp.float32)
        keep_cols = (cols < virtual_count[right]).astype(jnp.float32)
        denominator = (
            energy_rows[:, None]
            + energy_cols[None, :]
            - occupied_energy[left]
            - occupied_energy[right]
        )
        return term * keep_rows[:, None] * keep_cols[None, :] / denominator

    def join(part, other):
        return jnp.where(
            bit == 0,
            jnp.concatenate([part, other], 0),
            jnp.concatenate([other, part], 0),
        )

    def in_order(pieces):
        whole = jnp.zeros((X * QUARTER, pieces[0].shape[1]), jnp.float32)
        for r, piece in enumerate(pieces):
            whole = lax.dynamic_update_slice_in_dim(
                whole, piece, (px - r) % X * QUARTER, 0
            )
        return whole

    one, two, three = base, base + 1, (base + 2) % ORB

    other = move(own, SWAP)
    arrived = [move(own[c * ROWS : (c + 1) * ROWS], DOWN[c]) for c in (0, 1)]
    slab_one = jnp.where(first, own, other)
    slab_two = jnp.where(first, other, own)
    one_cols = cols_at(slab_one, at, COLS)
    two_cols = cols_at(slab_two, at, COLS)

    inner_sends = send_x(pair_term(slab_one, slab_two, two_cols, one_cols))
    inner_parts = around(inner_sends)

    near_two = rows_at(slab_two, core * ROWS, ROWS)
    far_two = rows_at(slab_two, (1 - core) * ROWS, ROWS)
    near_two_cols, far_two_cols = cols_at(near_two, at, COLS), cols_at(far_two, at, COLS)
    arrived = after(arrived, inner_parts, near_two, far_two, near_two_cols, far_two_cols)
    near = jnp.where(first, arrived[0], arrived[1])
    far = move(near, SWAP)
    near_cols = cols_at(near, at, COLS)
    outer_near = pair_term(near_two, near, near_cols, near_two_cols)
    far = after(far, outer_near)
    far_cols = cols_at(far, at, COLS)
    outer = outer_near + pair_term(far_two, far, far_cols, far_two_cols)
    outer_sends = send_x(outer)
    outer_parts = around(outer_sends)

    inner_kept, inner_sent = halves(add_x(after(inner_parts, outer_sends)))
    inner_kept = inner_kept + move(inner_sent, ALONG[1])
    inner_far = move(inner_kept, ALONG[2])

    outer_kept, outer_sent = halves(add_x(after(outer_parts, inner_kept)))
    outer_next = move(outer_sent, ALONG[1])
    inner_t = amplitude(inner_kept + after(inner_far, outer_sent), one, two, at)
    inner_other = move(inner_t, ALONG[1])
    outer_kept = outer_kept + after(outer_next, inner_t)
    outer_far = move(outer_kept, ALONG[2])
    inner_quarter = join(inner_t, after(inner_other, outer_kept))
    inner_pieces = around([inner_quarter] * X)
    outer_t = amplitude(outer_kept + after(outer_far, inner_quarter), two, three, at)
    outer_other = move(outer_t, ALONG[1])

    spans = [slice(w * CHUNK, (w + 1) * CHUNK) for w in range(COLS // CHUNK)]
    quarters = [join(outer_t[:, w], outer_other[:, w]) for w in spans]
    pieces = [around([q] * X) for q in quarters]
    outer_all, incoming, earlier = [], [[], []], quarters
    for n in range(len(spans)):
        outer_all.append(in_order(after(pieces[n], earlier)))
        outgoing = dot(slab_two, outer_all[n], 1, 0)
        for c in (0, 1):
            incoming[c].append(move(outgoing, UP[c]))
        earlier = outgoing

    inner_all = in_order(after(inner_pieces, outgoing))
    to_one = dot(two_cols, inner_all, 1, 1)
    to_two = dot(slab_one, inner_all, 1, 0)
    three_cols = jnp.where(
        first,
        jnp.concatenate([near_cols, far_cols], 0),
        jnp.concatenate([far_cols, near_cols], 0),
    )
    three_cols, outer_all = after((three_cols, outer_all), outgoing)
    beyond = sum(dot(three_cols[:, w], t, 1, 1) for w, t in zip(spans, outer_all))
    blank = jnp.zeros_like(to_two)
    to_two = beyond + jnp.where(
        first,
        jnp.concatenate([to_two, blank], 1),
        jnp.concatenate([blank, to_two], 1),
    )
    crossed = move(jnp.where(first, to_two, to_one), SWAP)
    density = jnp.where(first, to_one, to_two) + crossed
    incoming = after(incoming, density)
    density = density + jnp.concatenate(incoming[0] + incoming[1], 1)
    return density[None]


def solution(mesh):
    placed = (P("orb", "aux", None), P(), P(), P())
    return jax.shard_map(
        shards, mesh=mesh, in_specs=placed, out_specs=P("orb", "aux", None), check_vma=False
    )
```

```python
import jax
import jax.numpy as jnp
from jax import lax
from jax.sharding import PartitionSpec as P


ORB, AUX = 32, 16
AXES = ("orb", "aux")
X, ZL = 4, 4
QUARTER, HALF_Q, COLS = 256, 128, 512
ROWS, CHUNK = 256, 256


def route(step):
    pairs = []
    for orbital in range(ORB):
        for shard in range(AUX):
            target = step(orbital, shard // ZL, shard % ZL)
            if target is not None:
                o, x, z = target
                pairs.append((orbital * AUX + shard, o % ORB * AUX + x % X * ZL + z))
    return pairs


SWAP = route(lambda o, x, z: (o ^ 1, x, z))
DOWN = [route(lambda o, x, z: (o - 2 + c, x, z) if o % 2 == 0 else None) for c in (0, 1)]
UP = [route(lambda o, x, z: (o + 2 - c, x, z) if o % 2 == c else None) for c in (0, 1)]
AROUND = [route(lambda o, x, z: (o, x + r, z)) for r in range(X)]
ALONG = [route(lambda o, x, z: (o, x, z ^ d)) for d in range(ZL)]


def move(block, pairs):
    return lax.ppermute(block, AXES, pairs)


def dot(a, b, da, db):
    return lax.dot_general(
        a,
        b,
        (((da,), (db,)), ((), ())),
        precision=lax.Precision.HIGH,
        preferred_element_type=jnp.float32,
    )


def rows_at(block, start, size):
    return lax.dynamic_slice_in_dim(block, start, size, 0)


def cols_at(block, start, size):
    return lax.dynamic_slice_in_dim(block, start, size, 1)


def after(value, *earlier):
    return lax.optimization_barrier((value, earlier))[0]


def pair_term(one, two, two_cols, one_cols):
    return 2.0 * dot(one, two_cols, 0, 0) - dot(two, one_cols, 0, 0)


def shards(orbital_slabs, occupied_energy, virtual_energy, virtual_count):
    own = orbital_slabs[0]
    orbital = lax.axis_index("orb")
    shard = lax.axis_index("aux")
    core, base = orbital % 2, orbital - orbital % 2
    px, pz = shard // ZL, shard % ZL
    bit = pz % 2
    first = core == 0
    at = core * COLS

    def send_x(term):
        return [rows_at(term, (px + r) % X * QUARTER, QUARTER) for r in range(X)]

    def add_x(parts):
        return (parts[0] + parts[1]) + (parts[2] + parts[3])

    def around(parts):
        return [parts[0]] + [move(parts[r], AROUND[r]) for r in (1, 2, 3)]

    def halves(total):
        return rows_at(total, bit * HALF_Q, HALF_Q), rows_at(
            total, (1 - bit) * HALF_Q, HALF_Q
        )

    def weight(left, right, col):
        row = px * QUARTER + bit * HALF_Q
        rows = row + jnp.arange(HALF_Q, dtype=jnp.int32)
        cols = col + jnp.arange(COLS, dtype=jnp.int32)
        energy_rows = lax.dynamic_slice_in_dim(virtual_energy, row, HALF_Q)
        energy_cols = lax.dynamic_slice_in_dim(virtual_energy, col, COLS)
        keep_rows = (rows < virtual_count[left]).astype(jnp.float32)
        keep_cols = (cols < virtual_count[right]).astype(jnp.float32)
        denominator = (
            energy_rows[:, None]
            + energy_cols[None, :]
            - occupied_energy[left]
            - occupied_energy[right]
        )
        return keep_rows[:, None] * keep_cols[None, :] / denominator

    def join(part, other):
        return jnp.where(
            bit == 0,
            jnp.concatenate([part, other], 0),
            jnp.concatenate([other, part], 0),
        )

    def in_order(pieces):
        whole = jnp.zeros((X * QUARTER, pieces[0].shape[1]), jnp.float32)
        for r, piece in enumerate(pieces):
            whole = lax.dynamic_update_slice_in_dim(
                whole, piece, (px - r) % X * QUARTER, 0
            )
        return whole

    one, two, three = base, base + 1, (base + 2) % ORB

    other = move(own, SWAP)
    arrived = [move(own[c * ROWS : (c + 1) * ROWS], DOWN[c]) for c in (0, 1)]
    slab_one = jnp.where(first, own, other)
    slab_two = jnp.where(first, other, own)
    one_cols = cols_at(slab_one, at, COLS)
    two_cols = cols_at(slab_two, at, COLS)

    inner_sends = send_x(pair_term(slab_one, slab_two, two_cols, one_cols))
    inner_parts = around(inner_sends)

    near_two = rows_at(slab_two, core * ROWS, ROWS)
    far_two = rows_at(slab_two, (1 - core) * ROWS, ROWS)
    near_two_cols, far_two_cols = cols_at(near_two, at, COLS), cols_at(far_two, at, COLS)
    inner_weight, outer_weight = weight(one, two, at), weight(two, three, at)
    ready = (arrived, inner_weight, outer_weight)
    ready = after(ready, inner_parts, near_two, far_two, near_two_cols, far_two_cols)
    arrived, inner_weight, outer_weight = ready
    near = jnp.where(first, arrived[0], arrived[1])
    far = move(near, SWAP)
    near_cols = cols_at(near, at, COLS)
    outer_near = pair_term(near_two, near, near_cols, near_two_cols)
    far = after(far, outer_near)
    far_cols = cols_at(far, at, COLS)
    outer = outer_near + pair_term(far_two, far, far_cols, far_two_cols)
    outer_sends = send_x(outer)
    outer_parts = around(outer_sends)

    inner_kept, inner_sent = halves(add_x(after(inner_parts, outer_sends)))
    inner_kept = inner_kept + move(inner_sent, ALONG[1])
    inner_far = move(inner_kept, ALONG[2])

    outer_kept, outer_sent = halves(add_x(after(outer_parts, inner_kept)))
    outer_kept = outer_kept + move(outer_sent, ALONG[1])
    outer_far = move(outer_kept, ALONG[2])
    inner_t = (inner_kept + after(inner_far, outer_kept)) * inner_weight
    inner_other = move(inner_t, ALONG[1])
    outer_t = (outer_kept + after(outer_far, inner_t)) * outer_weight
    outer_other = move(outer_t, ALONG[1])
    inner_quarter = join(inner_t, after(inner_other, outer_t))
    inner_pieces = around([inner_quarter] * X)
    outer_other = after(outer_other, inner_quarter)

    spans = [slice(w * CHUNK, (w + 1) * CHUNK) for w in range(COLS // CHUNK)]
    quarters = [join(outer_t[:, w], outer_other[:, w]) for w in spans]
    pieces = [around([q] * X) for q in quarters]
    outer_all, incoming, earlier = [], [[], []], quarters
    for n in range(len(spans)):
        outer_all.append(in_order(after(pieces[n], earlier)))
        outgoing = dot(slab_two, outer_all[n], 1, 0)
        for c in (0, 1):
            incoming[c].append(move(outgoing, UP[c]))
        earlier = outgoing

    inner_all = in_order(after(inner_pieces, outgoing))
    to_one = dot(two_cols, inner_all, 1, 1)
    to_two = dot(slab_one, inner_all, 1, 0)
    three_cols = jnp.where(
        first,
        jnp.concatenate([near_cols, far_cols], 0),
        jnp.concatenate([far_cols, near_cols], 0),
    )
    three_cols, outer_all = after((three_cols, outer_all), outgoing)
    beyond = sum(dot(three_cols[:, w], t, 1, 1) for w, t in zip(spans, outer_all))
    blank = jnp.zeros_like(to_two)
    to_two = beyond + jnp.where(
        first,
        jnp.concatenate([to_two, blank], 1),
        jnp.concatenate([blank, to_two], 1),
    )
    crossed = move(jnp.where(first, to_two, to_one), SWAP)
    density = jnp.where(first, to_one, to_two) + crossed
    incoming = after(incoming, density)
    density = density + jnp.concatenate(incoming[0] + incoming[1], 1)
    return density[None]


def solution(mesh):
    placed = (P("orb", "aux", None), P(), P(), P())
    return jax.shard_map(
        shards, mesh=mesh, in_specs=placed, out_specs=P("orb", "aux", None), check_vma=False
    )
```

```python
import jax
import jax.numpy as jnp
from jax import lax
from jax.sharding import PartitionSpec as P


ORB, AUX = 32, 16
AXES = ("orb", "aux")
X, ZL = 4, 4
QUARTER, HALF_Q, COLS = 256, 128, 512
ROWS, CHUNK = 256, 256


def route(step):
    pairs = []
    for orbital in range(ORB):
        for shard in range(AUX):
            target = step(orbital, shard // ZL, shard % ZL)
            if target is not None:
                o, x, z = target
                pairs.append((orbital * AUX + shard, o % ORB * AUX + x % X * ZL + z))
    return pairs


SWAP = route(lambda o, x, z: (o ^ 1, x, z))
DOWN = [route(lambda o, x, z: (o - 2 + c, x, z) if o % 2 == 0 else None) for c in (0, 1)]
UP = [route(lambda o, x, z: (o + 2 - c, x, z) if o % 2 == c else None) for c in (0, 1)]
AROUND = [route(lambda o, x, z: (o, x + r, z)) for r in range(X)]
ALONG = [route(lambda o, x, z: (o, x, z ^ d)) for d in range(ZL)]


def move(block, pairs):
    return lax.ppermute(block, AXES, pairs)


def dot(a, b, da, db):
    return lax.dot_general(
        a,
        b,
        (((da,), (db,)), ((), ())),
        precision=lax.Precision.HIGH,
        preferred_element_type=jnp.float32,
    )


def rows_at(block, start, size):
    return lax.dynamic_slice_in_dim(block, start, size, 0)


def cols_at(block, start, size):
    return lax.dynamic_slice_in_dim(block, start, size, 1)


def after(value, *earlier):
    return lax.optimization_barrier((value, earlier))[0]


def pair_term(one, two, two_cols, one_cols):
    return 2.0 * dot(one, two_cols, 0, 0) - dot(two, one_cols, 0, 0)


def shards(orbital_slabs, occupied_energy, virtual_energy, virtual_count):
    own = orbital_slabs[0]
    orbital = lax.axis_index("orb")
    shard = lax.axis_index("aux")
    core, base = orbital % 2, orbital - orbital % 2
    px, pz = shard // ZL, shard % ZL
    bit = pz % 2
    first = core == 0
    at = core * COLS

    def send_x(term):
        return [rows_at(term, (px + r) % X * QUARTER, QUARTER) for r in range(X)]

    def add_x(parts):
        return (parts[0] + parts[1]) + (parts[2] + parts[3])

    def around(parts):
        return [parts[0]] + [move(parts[r], AROUND[r]) for r in (1, 2, 3)]

    def halves(total):
        return rows_at(total, bit * HALF_Q, HALF_Q), rows_at(
            total, (1 - bit) * HALF_Q, HALF_Q
        )

    def weight(left, right, col, occupied_energy, virtual_energy, virtual_count):
        row = px * QUARTER + bit * HALF_Q
        rows = row + jnp.arange(HALF_Q, dtype=jnp.int32)
        cols = col + jnp.arange(COLS, dtype=jnp.int32)
        energy_rows = lax.dynamic_slice_in_dim(virtual_energy, row, HALF_Q)
        energy_cols = lax.dynamic_slice_in_dim(virtual_energy, col, COLS)
        keep_rows = (rows < virtual_count[left]).astype(jnp.float32)
        keep_cols = (cols < virtual_count[right]).astype(jnp.float32)
        denominator = (
            energy_rows[:, None]
            + energy_cols[None, :]
            - occupied_energy[left]
            - occupied_energy[right]
        )
        return keep_rows[:, None] * keep_cols[None, :] / denominator

    def join(part, other):
        return jnp.where(
            bit == 0,
            jnp.concatenate([part, other], 0),
            jnp.concatenate([other, part], 0),
        )

    def in_order(pieces):
        whole = jnp.zeros((X * QUARTER, pieces[0].shape[1]), jnp.float32)
        for r, piece in enumerate(pieces):
            whole = lax.dynamic_update_slice_in_dim(
                whole, piece, (px - r) % X * QUARTER, 0
            )
        return whole

    one, two, three = base, base + 1, (base + 2) % ORB

    other = move(own, SWAP)
    arrived = [move(own[c * ROWS : (c + 1) * ROWS], DOWN[c]) for c in (0, 1)]
    slab_one = jnp.where(first, own, other)
    slab_two = jnp.where(first, other, own)
    one_cols = cols_at(slab_one, at, COLS)
    two_cols = cols_at(slab_two, at, COLS)

    inner_sends = send_x(pair_term(slab_one, slab_two, two_cols, one_cols))
    inner_parts = around(inner_sends)
    energies = after((occupied_energy, virtual_energy, virtual_count), inner_sends)
    inner_weight = weight(one, two, at, *energies)
    outer_weight = weight(two, three, at, *energies)
    near_two = rows_at(slab_two, core * ROWS, ROWS)
    far_two = rows_at(slab_two, (1 - core) * ROWS, ROWS)
    near_two_cols, far_two_cols = cols_at(near_two, at, COLS), cols_at(far_two, at, COLS)
    prepared = (near_two, far_two, near_two_cols, far_two_cols)
    ready = after((inner_parts, inner_weight, outer_weight), prepared)
    inner_parts, inner_weight, outer_weight = ready
    inner_kept, inner_sent = halves(add_x(inner_parts))
    inner_next = move(inner_sent, ALONG[1])

    arrived = after(arrived, inner_sent)
    near = arrived[0] + arrived[1]
    far = move(near, SWAP)
    near_cols = cols_at(near, at, COLS)
    outer_near = pair_term(near_two, near, near_cols, near_two_cols)
    far = after(far, outer_near)
    far_cols = cols_at(far, at, COLS)
    outer = outer_near + pair_term(far_two, far, far_cols, far_two_cols)

    left, right = slice(0, CHUNK), slice(CHUNK, COLS)
    sends = [send_x(outer[:, w]) for w in (left, right)]
    parts = [around(sends[n]) for n in (0, 1)]
    inner_kept = inner_kept + after(inner_next, sends)
    inner_far = move(inner_kept, ALONG[2])

    kept_a, sent_a = halves(add_x(after(parts[0], inner_kept)))
    kept_a = kept_a + move(sent_a, ALONG[1])
    far_a = move(kept_a, ALONG[2])
    kept_b, sent_b = halves(add_x(after(parts[1], kept_a)))
    next_b = move(sent_b, ALONG[1])

    inner_t = (inner_kept + after(inner_far, sent_b)) * inner_weight
    inner_other = move(inner_t, ALONG[1])
    t_a = (kept_a + after(far_a, inner_t)) * outer_weight[:, left]
    other_a = move(t_a, ALONG[1])
    kept_b = kept_b + after(next_b, t_a)
    far_b = move(kept_b, ALONG[2])

    quarter_a = join(t_a, after(other_a, kept_b))
    pieces_a = around([quarter_a] * X)
    inner_quarter = join(inner_t, after(inner_other, quarter_a))
    inner_pieces = around([inner_quarter] * X)
    t_b = (kept_b + after(far_b, inner_quarter)) * outer_weight[:, right]
    other_b = move(t_b, ALONG[1])

    all_a = in_order(after(pieces_a, t_b))
    leaving_a = dot(slab_two, all_a, 1, 0)
    incoming_a = [move(leaving_a, UP[c]) for c in (0, 1)]
    quarter_b = join(t_b, after(other_b, leaving_a))
    pieces_b = around([quarter_b] * X)
    all_b = in_order(pieces_b)
    outgoing = dot(slab_two, all_b, 1, 0)
    incoming_b = [move(outgoing, UP[c]) for c in (0, 1)]
    incoming = [incoming_a[0], incoming_b[0], incoming_a[1], incoming_b[1]]

    inner_all = in_order(after(inner_pieces, outgoing))
    to_one = dot(two_cols, inner_all, 1, 1)
    to_two = dot(slab_one, inner_all, 1, 0)
    three_cols = jnp.where(
        first,
        jnp.concatenate([near_cols, far_cols], 0),
        jnp.concatenate([far_cols, near_cols], 0),
    )
    three_cols, all_a, all_b = after((three_cols, all_a, all_b), outgoing)
    beyond = dot(three_cols[:, left], all_a, 1, 1) + dot(three_cols[:, right], all_b, 1, 1)
    blank = jnp.zeros_like(to_two)
    to_two = beyond + jnp.where(
        first,
        jnp.concatenate([to_two, blank], 1),
        jnp.concatenate([blank, to_two], 1),
    )
    crossed = move(jnp.where(first, to_two, to_one), SWAP)
    density = jnp.where(first, to_one, to_two) + crossed
    incoming = after(incoming, density)
    density = density + jnp.concatenate(incoming, 1)
    return density[None]


def solution(mesh):
    placed = (P("orb", "aux", None), P(), P(), P())
    return jax.shard_map(
        shards, mesh=mesh, in_specs=placed, out_specs=P("orb", "aux", None), check_vma=False
    )
```

```python
import jax
import jax.numpy as jnp
from jax import lax
from jax.sharding import PartitionSpec as P


ORB, AUX = 32, 16
AXES = ("orb", "aux")
X, ZL = 4, 4
QUARTER, HALF_Q, COLS = 256, 128, 512
ROWS, CHUNK = 256, 256


def route(step):
    pairs = []
    for orbital in range(ORB):
        for shard in range(AUX):
            target = step(orbital, shard // ZL, shard % ZL)
            if target is not None:
                o, x, z = target
                pairs.append((orbital * AUX + shard, o % ORB * AUX + x % X * ZL + z))
    return pairs


SWAP = route(lambda o, x, z: (o ^ 1, x, z))
DOWN = route(lambda o, x, z: (o - 2, x, z))
UP = [route(lambda o, x, z: (o + 2 - c, x, z) if o % 2 == c else None) for c in (0, 1)]
AROUND = [route(lambda o, x, z: (o, x + r, z)) for r in range(X)]
ACROSS = [route(lambda o, x, z: (o, x ^ d, z)) for d in range(X)]
ALONG = [route(lambda o, x, z: (o, x, z ^ d)) for d in range(ZL)]


def move(block, pairs):
    return lax.ppermute(block, AXES, pairs)


def dot(a, b, da, db):
    return lax.dot_general(
        a,
        b,
        (((da,), (db,)), ((), ())),
        precision=lax.Precision.HIGH,
        preferred_element_type=jnp.float32,
    )


def rows_at(block, start, size):
    return lax.dynamic_slice_in_dim(block, start, size, 0)


def cols_at(block, start, size):
    return lax.dynamic_slice_in_dim(block, start, size, 1)


def after(value, *earlier):
    return lax.optimization_barrier((value, earlier))[0]


def pair_term(one, two, two_cols, one_cols):
    return 2.0 * dot(one, two_cols, 0, 0) - dot(two, one_cols, 0, 0)


def shards(orbital_slabs, occupied_energy, virtual_energy, virtual_count):
    own = orbital_slabs[0]
    orbital = lax.axis_index("orb")
    shard = lax.axis_index("aux")
    core, base = orbital % 2, orbital - orbital % 2
    px, pz = shard // ZL, shard % ZL
    bit = pz % 2
    first = core == 0
    at = core * COLS

    def send_x(term):
        return [rows_at(term, (px + r) % X * QUARTER, QUARTER) for r in range(X)]

    def add_x(parts):
        return (parts[0] + parts[1]) + (parts[2] + parts[3])

    def around(parts):
        return [parts[0]] + [move(parts[r], AROUND[r]) for r in (1, 2, 3)]

    def halves(total):
        return rows_at(total, bit * HALF_Q, HALF_Q), rows_at(
            total, (1 - bit) * HALF_Q, HALF_Q
        )

    def weight(left, right, col, occupied_energy, virtual_energy, virtual_count):
        row = px * QUARTER + bit * HALF_Q
        rows = row + jnp.arange(HALF_Q, dtype=jnp.int32)
        cols = col + jnp.arange(COLS, dtype=jnp.int32)
        energy_rows = lax.dynamic_slice_in_dim(virtual_energy, row, HALF_Q)
        energy_cols = lax.dynamic_slice_in_dim(virtual_energy, col, COLS)
        keep_rows = (rows < virtual_count[left]).astype(jnp.float32)
        keep_cols = (cols < virtual_count[right]).astype(jnp.float32)
        denominator = (
            energy_rows[:, None]
            + energy_cols[None, :]
            - occupied_energy[left]
            - occupied_energy[right]
        )
        return keep_rows[:, None] * keep_cols[None, :] / denominator

    def join(part, other):
        return jnp.where(
            bit == 0,
            jnp.concatenate([part, other], 0),
            jnp.concatenate([other, part], 0),
        )

    def place(whole, piece, quarter):
        return lax.dynamic_update_slice_in_dim(whole, piece, quarter * QUARTER, 0)

    def in_order(pieces):
        whole = jnp.zeros((X * QUARTER, pieces[0].shape[1]), jnp.float32)
        for r, piece in enumerate(pieces):
            whole = place(whole, piece, (px - r) % X)
        return whole

    one, two, three = base, base + 1, (base + 2) % ORB

    other = move(own, SWAP)
    slab_one = jnp.where(first, own, other)
    slab_two = jnp.where(first, other, own)
    near = move(rows_at(slab_one, core * ROWS, ROWS), DOWN)
    one_cols = cols_at(slab_one, at, COLS)
    two_cols = cols_at(slab_two, at, COLS)

    inner = pair_term(slab_one, slab_two, two_cols, one_cols)
    inner_sends = send_x(inner)
    inner_parts = around(inner_sends)
    energies = after((occupied_energy, virtual_energy, virtual_count), inner_sends)
    inner_weight = weight(one, two, at, *energies)
    outer_weight = weight(two, three, at, *energies)
    near_two = rows_at(slab_two, core * ROWS, ROWS)
    far_two = rows_at(slab_two, (1 - core) * ROWS, ROWS)
    near_two_cols, far_two_cols = cols_at(near_two, at, COLS), cols_at(far_two, at, COLS)
    prepared = (near_two, far_two, near_two_cols, far_two_cols)
    ready = after((inner_parts, inner_weight, outer_weight), prepared)
    inner_parts, inner_weight, outer_weight = ready
    inner_kept, inner_sent = halves(add_x(inner_parts))
    inner_next = move(inner_sent, ALONG[1])

    near = after(near, inner_sent)
    far = move(near, SWAP)
    near_cols = cols_at(near, at, COLS)
    outer_near = pair_term(near_two, near, near_cols, near_two_cols)
    far = after(far, outer_near)
    far_cols = cols_at(far, at, COLS)
    outer = outer_near + pair_term(far_two, far, far_cols, far_two_cols)

    left, right = slice(0, CHUNK), slice(CHUNK, COLS)
    sends = [send_x(outer[:, w]) for w in (left, right)]
    parts = [around(sends[n]) for n in (0, 1)]
    inner_kept = inner_kept + after(inner_next, sends[0])
    inner_far = move(inner_kept, ALONG[2])

    kept_a, sent_a = halves(add_x(after(parts[0], sends, inner_kept)))
    next_a = move(sent_a, ALONG[1])
    held_near, held_far = after((near_cols, far_cols), sent_a)
    three_cols = jnp.where(
        first,
        jnp.concatenate([held_near, held_far], 0),
        jnp.concatenate([held_far, held_near], 0),
    )
    inner_far, three_cols = after((inner_far, three_cols), sent_a)
    inner_t = (inner_kept + inner_far) * inner_weight
    inner_other = move(inner_t, ALONG[1])
    kept_a = kept_a + after(next_a, inner_t)
    far_a = move(kept_a, ALONG[2])
    parts_b = after(parts[1], kept_a)
    sum_b = add_x(parts_b)
    kept_b, sent_b = halves(sum_b)
    next_b = move(sent_b, ALONG[1])
    inner_quarter = join(inner_t, after(inner_other, sent_b))
    inner_next = move(inner_quarter, ACROSS[1])

    t_a = (kept_a + after(far_a, inner_quarter)) * outer_weight[:, left]
    other_a = move(t_a, ALONG[1])
    kept_b = kept_b + after(next_b, t_a)
    far_b = move(kept_b, ALONG[2])
    quarter_a = join(t_a, after(other_a, kept_b))
    pieces_a = around([quarter_a] * X)
    t_b = (kept_b + after(far_b, quarter_a)) * outer_weight[:, right]
    other_b = move(t_b, ALONG[1])
    inner_pair = jnp.concatenate([inner_quarter, after(inner_next, t_b)], 0)
    inner_rest = move(inner_pair, ACROSS[3])

    inner_all = jnp.zeros((X * QUARTER, COLS), jnp.float32)
    inner_all = place(inner_all, inner_pair[:QUARTER], px)
    inner_all = place(inner_all, inner_pair[QUARTER:], px ^ 1)
    all_a = in_order(after(pieces_a, t_b, inner_all))
    leaving_a = dot(slab_two, all_a, 1, 0)
    incoming_a = [move(leaving_a, UP[c]) for c in (0, 1)]
    quarter_b = join(t_b, after(other_b, leaving_a))
    pieces_b = around([quarter_b] * X)
    all_b = in_order(pieces_b)
    outgoing = dot(slab_two, all_b, 1, 0)
    incoming_b = [move(outgoing, UP[c]) for c in (0, 1)]
    incoming = [incoming_a[0], incoming_b[0], incoming_a[1], incoming_b[1]]

    inner_rest = after(inner_rest, outgoing)
    inner_all = place(inner_all, inner_rest[:QUARTER], px ^ 3)
    inner_all = place(inner_all, inner_rest[QUARTER:], px ^ 2)
    to_one = dot(two_cols, inner_all, 1, 1)
    to_two = dot(slab_one, inner_all, 1, 0)
    three_cols, all_a, all_b = after((three_cols, all_a, all_b), outgoing)
    beyond = dot(three_cols[:, left], all_a, 1, 1) + dot(three_cols[:, right], all_b, 1, 1)
    blank = jnp.zeros_like(to_two)
    to_two = beyond + jnp.where(
        first,
        jnp.concatenate([to_two, blank], 1),
        jnp.concatenate([blank, to_two], 1),
    )
    crossed = move(jnp.where(first, to_two, to_one), SWAP)
    crossed, incoming = after((crossed, incoming))
    density = jnp.where(first, to_one, to_two) + crossed + jnp.concatenate(incoming, 1)
    return density[None]


def solution(mesh):
    placed = (P("orb", "aux", None), P(), P(), P())
    return jax.shard_map(
        shards, mesh=mesh, in_specs=placed, out_specs=P("orb", "aux", None), check_vma=False
    )
```

```python
import jax
import jax.numpy as jnp
from jax import lax
from jax.sharding import PartitionSpec as P


ORB, AUX = 32, 16
AXES = ("orb", "aux")
X, ZL = 4, 4
QUARTER, HALF_Q, COLS = 256, 128, 512
ROWS, CHUNK = 256, 256


def route(step):
    pairs = []
    for orbital in range(ORB):
        for shard in range(AUX):
            target = step(orbital, shard // ZL, shard % ZL)
            if target is not None:
                o, x, z = target
                pairs.append((orbital * AUX + shard, o % ORB * AUX + x % X * ZL + z))
    return pairs


SWAP = route(lambda o, x, z: (o ^ 1, x, z))
DOWN = route(lambda o, x, z: (o - 2, x, z))
UP = [route(lambda o, x, z: (o + 2 - c, x, z) if o % 2 == c else None) for c in (0, 1)]
AROUND = [route(lambda o, x, z: (o, x + r, z)) for r in range(X)]
ACROSS = [route(lambda o, x, z: (o, x ^ d, z)) for d in range(X)]
ALONG = [route(lambda o, x, z: (o, x, z ^ d)) for d in range(ZL)]


def move(block, pairs):
    return lax.ppermute(block, AXES, pairs)


def dot(a, b, da, db):
    return lax.dot_general(
        a,
        b,
        (((da,), (db,)), ((), ())),
        precision=lax.Precision.HIGH,
        preferred_element_type=jnp.float32,
    )


def rows_at(block, start, size):
    return lax.dynamic_slice_in_dim(block, start, size, 0)


def cols_at(block, start, size):
    return lax.dynamic_slice_in_dim(block, start, size, 1)


def after(value, *earlier):
    return lax.optimization_barrier((value, earlier))[0]


def pair_term(one, two, two_cols, one_cols):
    return 2.0 * dot(one, two_cols, 0, 0) - dot(two, one_cols, 0, 0)


def shards(orbital_slabs, occupied_energy, virtual_energy, virtual_count):
    own = orbital_slabs[0]
    orbital = lax.axis_index("orb")
    shard = lax.axis_index("aux")
    core, base = orbital % 2, orbital - orbital % 2
    px, pz = shard // ZL, shard % ZL
    bit = pz % 2
    first = core == 0
    at = core * COLS

    def send_x(term):
        return [rows_at(term, (px + r) % X * QUARTER, QUARTER) for r in range(X)]

    def add_x(parts):
        return (parts[0] + parts[1]) + (parts[2] + parts[3])

    def around(parts):
        return [parts[0]] + [move(parts[r], AROUND[r]) for r in (1, 2, 3)]

    def halves(total):
        return rows_at(total, bit * HALF_Q, HALF_Q), rows_at(
            total, (1 - bit) * HALF_Q, HALF_Q
        )

    def weight(left, right, row, height, col, occupied_energy, virtual_energy, virtual_count):
        rows = row + jnp.arange(height, dtype=jnp.int32)
        cols = col + jnp.arange(COLS, dtype=jnp.int32)
        energy_rows = lax.dynamic_slice_in_dim(virtual_energy, row, height)
        energy_cols = lax.dynamic_slice_in_dim(virtual_energy, col, COLS)
        keep_rows = (rows < virtual_count[left]).astype(jnp.float32)
        keep_cols = (cols < virtual_count[right]).astype(jnp.float32)
        denominator = (
            energy_rows[:, None]
            + energy_cols[None, :]
            - occupied_energy[left]
            - occupied_energy[right]
        )
        return keep_rows[:, None] * keep_cols[None, :] / denominator

    def join(part, other):
        return jnp.where(
            bit == 0,
            jnp.concatenate([part, other], 0),
            jnp.concatenate([other, part], 0),
        )

    def in_order(pieces):
        whole = jnp.zeros((X * QUARTER, pieces[0].shape[1]), jnp.float32)
        for r, piece in enumerate(pieces):
            whole = lax.dynamic_update_slice_in_dim(
                whole, piece, (px - r) % X * QUARTER, 0
            )
        return whole

    one, two, three = base, base + 1, (base + 2) % ORB

    other = move(own, SWAP)
    slab_one = jnp.where(first, own, other)
    slab_two = jnp.where(first, other, own)
    near = move(rows_at(slab_one, core * ROWS, ROWS), DOWN)
    one_cols = cols_at(slab_one, at, COLS)
    two_cols = cols_at(slab_two, at, COLS)

    inner = pair_term(slab_one, slab_two, two_cols, one_cols)
    inner_sends = send_x(inner)
    inner_parts = around(inner_sends)
    energies = after((occupied_energy, virtual_energy, virtual_count), inner_sends)
    row = px * QUARTER
    inner_weight = weight(one, two, row + bit * HALF_Q, HALF_Q, at, *energies)
    outer_weight = weight(two, three, row, QUARTER, at, *energies)
    near_two = rows_at(slab_two, core * ROWS, ROWS)
    far_two = rows_at(slab_two, (1 - core) * ROWS, ROWS)
    near_two_cols, far_two_cols = cols_at(near_two, at, COLS), cols_at(far_two, at, COLS)
    prepared = (near_two, far_two, near_two_cols, far_two_cols)
    ready = after((inner_parts, inner_weight, outer_weight), prepared)
    inner_parts, inner_weight, outer_weight = ready
    inner_kept, inner_sent = halves(add_x(inner_parts))
    inner_next = move(inner_sent, ALONG[1])

    near = after(near, inner_sent)
    far = move(near, SWAP)
    near_cols = cols_at(near, at, COLS)
    outer_near = pair_term(near_two, near, near_cols, near_two_cols)
    far = after(far, outer_near)
    far_cols = cols_at(far, at, COLS)
    outer = outer_near + pair_term(far_two, far, far_cols, far_two_cols)

    left, right = slice(0, CHUNK), slice(CHUNK, COLS)
    sends = [send_x(outer[:, w]) for w in (left, right)]
    parts = [around(sends[n]) for n in (0, 1)]
    kept_a = add_x(after(parts[0], sends))
    next_a = move(kept_a, ALONG[1])
    inner_kept = inner_kept + after(inner_next, kept_a)
    kept_a = kept_a + after(next_a, inner_kept)
    far_a = move(kept_a, ALONG[2])
    inner_far = move(inner_kept, ALONG[2])
    parts_b = after(parts[1], kept_a)
    kept_b = add_x(parts_b)
    next_b = move(kept_b, ALONG[1])

    quarter_a = (kept_a + after(far_a, kept_b)) * outer_weight[:, left]
    pieces_a = around([quarter_a] * X)
    inner_t = (inner_kept + after(inner_far, quarter_a)) * inner_weight
    inner_other = move(inner_t, ALONG[1])
    kept_b = kept_b + after(next_b, inner_t)
    far_b = move(kept_b, ALONG[2])
    inner_quarter = join(inner_t, after(inner_other, kept_b))
    inner_next = move(inner_quarter, ACROSS[1])

    all_a = in_order(after(pieces_a, inner_quarter))
    leaving_a = dot(slab_two, all_a, 1, 0)
    incoming_a = [move(leaving_a, UP[c]) for c in (0, 1)]
    held_weight = after(outer_weight, leaving_a)
    weight_b = held_weight[:, right]
    far_b, weight_b = after((far_b, weight_b))
    quarter_b = (kept_b + far_b) * weight_b
    pieces_b = around([quarter_b] * X)
    inner_pair = jnp.concatenate([inner_quarter, after(inner_next, quarter_b)], 0)
    inner_rest = move(inner_pair, ACROSS[3])
    all_b = in_order(after(pieces_b, inner_pair))
    outgoing = dot(slab_two, all_b, 1, 0)
    incoming_b = [move(outgoing, UP[c]) for c in (0, 1)]
    incoming = [incoming_a[0], incoming_b[0], incoming_a[1], incoming_b[1]]

    inner_all = jnp.zeros((X * QUARTER, COLS), jnp.float32)
    inner_rest = after(inner_rest, outgoing)
    for q, d in ((inner_pair, 0), (inner_rest, 3)):
        for part, e in ((q[:QUARTER], d), (q[QUARTER:], d ^ 1)):
            inner_all = lax.dynamic_update_slice_in_dim(
                inner_all, part, (px ^ e) * QUARTER, 0
            )
    to_one = dot(two_cols, inner_all, 1, 1)
    to_two = dot(slab_one, inner_all, 1, 0)
    three_cols = jnp.where(
        first,
        jnp.concatenate([near_cols, far_cols], 0),
        jnp.concatenate([far_cols, near_cols], 0),
    )
    three_cols, all_a, all_b = after((three_cols, all_a, all_b), outgoing)
    beyond = dot(three_cols[:, left], all_a, 1, 1) + dot(three_cols[:, right], all_b, 1, 1)
    blank = jnp.zeros_like(to_two)
    to_two = beyond + jnp.where(
        first,
        jnp.concatenate([to_two, blank], 1),
        jnp.concatenate([blank, to_two], 1),
    )
    crossed = move(jnp.where(first, to_two, to_one), SWAP)
    crossed, incoming = after((crossed, incoming))
    density = jnp.where(first, to_one, to_two) + crossed + jnp.concatenate(incoming, 1)
    return density[None]


def solution(mesh):
    placed = (P("orb", "aux", None), P(), P(), P())
    return jax.shard_map(
        shards, mesh=mesh, in_specs=placed, out_specs=P("orb", "aux", None), check_vma=False
    )
```

```python
import jax
import jax.numpy as jnp
from jax import lax
from jax.sharding import PartitionSpec as P


ORB, AUX = 32, 16
AXES = ("orb", "aux")
X, ZL = 4, 4
QUARTER, HALF_Q, COLS = 256, 128, 512
ROWS, CHUNK = 256, 256


def route(step):
    pairs = []
    for orbital in range(ORB):
        for shard in range(AUX):
            target = step(orbital, shard // ZL, shard % ZL)
            if target is not None:
                o, x, z = target
                pairs.append((orbital * AUX + shard, o % ORB * AUX + x % X * ZL + z))
    return pairs


SWAP = route(lambda o, x, z: (o ^ 1, x, z))
DOWN = route(lambda o, x, z: (o - 2, x, z))
UP = [route(lambda o, x, z: (o + 2 - c, x, z) if o % 2 == c else None) for c in (0, 1)]
AROUND = [route(lambda o, x, z: (o, x + r, z)) for r in range(X)]
ACROSS = [route(lambda o, x, z: (o, x ^ d, z)) for d in range(X)]
ALONG = [route(lambda o, x, z: (o, x, z ^ d)) for d in range(ZL)]


def move(block, pairs):
    return lax.ppermute(block, AXES, pairs)


def dot(a, b, da, db):
    return lax.dot_general(
        a,
        b,
        (((da,), (db,)), ((), ())),
        precision=lax.Precision.HIGH,
        preferred_element_type=jnp.float32,
    )


def rows_at(block, start, size):
    return lax.dynamic_slice_in_dim(block, start, size, 0)


def cols_at(block, start, size):
    return lax.dynamic_slice_in_dim(block, start, size, 1)


def after(value, *earlier):
    return lax.optimization_barrier((value, earlier))[0]


def pair_term(one, two, two_cols, one_cols):
    return 2.0 * dot(one, two_cols, 0, 0) - dot(two, one_cols, 0, 0)


def shards(orbital_slabs, occupied_energy, virtual_energy, virtual_count):
    own = orbital_slabs[0]
    orbital = lax.axis_index("orb")
    shard = lax.axis_index("aux")
    core, base = orbital % 2, orbital - orbital % 2
    px, pz = shard // ZL, shard % ZL
    bit = pz % 2
    first = core == 0
    at = core * COLS

    def send_x(term):
        return [rows_at(term, (px + r) % X * QUARTER, QUARTER) for r in range(X)]

    def add_x(parts):
        return (parts[0] + parts[1]) + (parts[2] + parts[3])

    def around(parts):
        return [parts[0]] + [move(parts[r], AROUND[r]) for r in (1, 2, 3)]

    def halves(total):
        return rows_at(total, bit * HALF_Q, HALF_Q), rows_at(
            total, (1 - bit) * HALF_Q, HALF_Q
        )

    def weight(left, right, row, height, col, occupied_energy, virtual_energy, virtual_count):
        rows = row + jnp.arange(height, dtype=jnp.int32)
        cols = col + jnp.arange(COLS, dtype=jnp.int32)
        energy_rows = lax.dynamic_slice_in_dim(virtual_energy, row, height)
        energy_cols = lax.dynamic_slice_in_dim(virtual_energy, col, COLS)
        keep_rows = (rows < virtual_count[left]).astype(jnp.float32)
        keep_cols = (cols < virtual_count[right]).astype(jnp.float32)
        denominator = (
            energy_rows[:, None]
            + energy_cols[None, :]
            - occupied_energy[left]
            - occupied_energy[right]
        )
        return keep_rows[:, None] * keep_cols[None, :] / denominator

    def join(part, other):
        return jnp.where(
            bit == 0,
            jnp.concatenate([part, other], 0),
            jnp.concatenate([other, part], 0),
        )

    def place(whole, piece, quarter):
        return lax.dynamic_update_slice_in_dim(whole, piece, quarter * QUARTER, 0)

    def in_order(pieces):
        whole = jnp.zeros((X * QUARTER, pieces[0].shape[1]), jnp.float32)
        for r, piece in enumerate(pieces):
            whole = place(whole, piece, (px - r) % X)
        return whole

    one, two, three = base, base + 1, (base + 2) % ORB

    other = move(own, SWAP)
    slab_one = jnp.where(first, own, other)
    slab_two = jnp.where(first, other, own)
    near = move(rows_at(slab_one, core * ROWS, ROWS), DOWN)
    one_cols = cols_at(slab_one, at, COLS)
    two_cols = cols_at(slab_two, at, COLS)

    inner = pair_term(slab_one, slab_two, two_cols, one_cols)
    inner_sends = send_x(inner)
    inner_parts = around(inner_sends)
    energies = after((occupied_energy, virtual_energy, virtual_count), inner_sends)
    row = px * QUARTER
    inner_weight = weight(one, two, row + bit * HALF_Q, HALF_Q, at, *energies)
    outer_weight = weight(two, three, row, QUARTER, at, *energies)
    near_two = rows_at(slab_two, core * ROWS, ROWS)
    far_two = rows_at(slab_two, (1 - core) * ROWS, ROWS)
    near_two_cols, far_two_cols = cols_at(near_two, at, COLS), cols_at(far_two, at, COLS)
    prepared = (near_two, far_two, near_two_cols, far_two_cols)
    ready = after((inner_parts, inner_weight, outer_weight), prepared)
    inner_parts, inner_weight, outer_weight = ready
    inner_kept, inner_sent = halves(add_x(inner_parts))
    inner_next = move(inner_sent, ALONG[1])

    near = after(near, inner_sent)
    far = move(near, SWAP)
    near_cols = cols_at(near, at, COLS)
    outer_near = pair_term(near_two, near, near_cols, near_two_cols)
    far = after(far, outer_near)
    far_cols = cols_at(far, at, COLS)
    outer = outer_near + pair_term(far_two, far, far_cols, far_two_cols)

    left, right = slice(0, CHUNK), slice(CHUNK, COLS)
    sends = [send_x(outer[:, w]) for w in (left, right)]
    parts = [around(sends[n]) for n in (0, 1)]
    inner_kept = inner_kept + after(inner_next, sends[0])
    inner_far = move(inner_kept, ALONG[2])

    kept_a = add_x(after(parts[0], sends, inner_kept))
    next_a = move(kept_a, ALONG[1])
    held_weight = after(outer_weight, kept_a)
    weight_a = held_weight[:, left]
    inner_far, weight_a = after((inner_far, weight_a))
    inner_t = (inner_kept + inner_far) * inner_weight
    inner_other = move(inner_t, ALONG[1])
    kept_a = kept_a + after(next_a, inner_t)
    far_a = move(kept_a, ALONG[2])
    parts_b = after(parts[1], kept_a)
    kept_b = add_x(parts_b)
    next_b = move(kept_b, ALONG[1])
    inner_quarter = join(inner_t, after(inner_other, kept_b))
    inner_next = move(inner_quarter, ACROSS[1])

    quarter_a = (kept_a + after(far_a, inner_quarter)) * weight_a
    pieces_a = around([quarter_a] * X)
    kept_b = kept_b + after(next_b, quarter_a)
    far_b = move(kept_b, ALONG[2])

    all_a = in_order(after(pieces_a, kept_b))
    leaving_a = dot(slab_two, all_a, 1, 0)
    incoming_a = [move(leaving_a, UP[c]) for c in (0, 1)]
    held_weight = after(outer_weight, leaving_a)
    weight_b = held_weight[:, right]
    far_b, weight_b = after((far_b, weight_b))
    quarter_b = (kept_b + far_b) * weight_b
    pieces_b = around([quarter_b] * X)
    inner_pair = jnp.concatenate([inner_quarter, after(inner_next, quarter_b)], 0)
    inner_rest = move(inner_pair, ACROSS[3])
    all_b = in_order(after(pieces_b, inner_pair))
    outgoing = dot(slab_two, all_b, 1, 0)
    incoming_b = [move(outgoing, UP[c]) for c in (0, 1)]
    incoming = [incoming_a[0], incoming_b[0], incoming_a[1], incoming_b[1]]

    inner_all = jnp.zeros((X * QUARTER, COLS), jnp.float32)
    inner_pair = after(inner_pair, outgoing)
    inner_all = place(inner_all, inner_pair[:QUARTER], px)
    inner_all = place(inner_all, inner_pair[QUARTER:], px ^ 1)
    inner_rest = after(inner_rest, inner_all)
    inner_all = place(inner_all, inner_rest[:QUARTER], px ^ 3)
    inner_all = place(inner_all, inner_rest[QUARTER:], px ^ 2)
    to_one = dot(two_cols, inner_all, 1, 1)
    to_two = dot(slab_one, inner_all, 1, 0)
    three_cols = jnp.where(
        first,
        jnp.concatenate([near_cols, far_cols], 0),
        jnp.concatenate([far_cols, near_cols], 0),
    )
    three_cols, all_a, all_b = after((three_cols, all_a, all_b), outgoing)
    beyond = dot(three_cols[:, left], all_a, 1, 1) + dot(three_cols[:, right], all_b, 1, 1)
    blank = jnp.zeros_like(to_two)
    to_two = beyond + jnp.where(
        first,
        jnp.concatenate([to_two, blank], 1),
        jnp.concatenate([blank, to_two], 1),
    )
    crossed = move(jnp.where(first, to_two, to_one), SWAP)
    crossed, incoming = after((crossed, incoming))
    density = jnp.where(first, to_one, to_two) + crossed + jnp.concatenate(incoming, 1)
    return density[None]


def solution(mesh):
    placed = (P("orb", "aux", None), P(), P(), P())
    return jax.shard_map(
        shards, mesh=mesh, in_specs=placed, out_specs=P("orb", "aux", None), check_vma=False
    )
```

```python
import jax
import jax.numpy as jnp
from jax import lax
from jax.sharding import PartitionSpec as P


ORB, AUX = 32, 16
AXES = ("orb", "aux")
X, ZL = 4, 4
QUARTER, HALF_Q, COLS = 256, 128, 512
ROWS, CHUNK = 256, 256


def route(step):
    pairs = []
    for orbital in range(ORB):
        for shard in range(AUX):
            target = step(orbital, shard // ZL, shard % ZL)
            if target is not None:
                o, x, z = target
                pairs.append((orbital * AUX + shard, o % ORB * AUX + x % X * ZL + z))
    return pairs


SWAP = route(lambda o, x, z: (o ^ 1, x, z))
DOWN = route(lambda o, x, z: (o - 2, x, z))
UP = [route(lambda o, x, z: (o + 2 - c, x, z) if o % 2 == c else None) for c in (0, 1)]
AROUND = [route(lambda o, x, z: (o, x + r, z)) for r in range(X)]
ACROSS = [route(lambda o, x, z: (o, x ^ d, z)) for d in range(X)]
ALONG = [route(lambda o, x, z: (o, x, z ^ d)) for d in range(ZL)]


def move(block, pairs):
    return lax.ppermute(block, AXES, pairs)


def dot(a, b, da, db):
    return lax.dot_general(
        a,
        b,
        (((da,), (db,)), ((), ())),
        precision=lax.Precision.HIGH,
        preferred_element_type=jnp.float32,
    )


def rows_at(block, start, size):
    return lax.dynamic_slice_in_dim(block, start, size, 0)


def cols_at(block, start, size):
    return lax.dynamic_slice_in_dim(block, start, size, 1)


def after(value, *earlier):
    return lax.optimization_barrier((value, earlier))[0]


def pair_term(one, two, two_cols, one_cols):
    return 2.0 * dot(one, two_cols, 0, 0) - dot(two, one_cols, 0, 0)


def shards(orbital_slabs, occupied_energy, virtual_energy, virtual_count):
    own = orbital_slabs[0]
    orbital = lax.axis_index("orb")
    shard = lax.axis_index("aux")
    core, base = orbital % 2, orbital - orbital % 2
    px, pz = shard // ZL, shard % ZL
    bit = pz % 2
    first = core == 0
    at = core * COLS

    def send_x(term):
        return [rows_at(term, (px + r) % X * QUARTER, QUARTER) for r in range(X)]

    def add_x(parts):
        return (parts[0] + parts[1]) + (parts[2] + parts[3])

    def around(parts):
        return [parts[0]] + [move(parts[r], AROUND[r]) for r in (1, 2, 3)]

    def halves(total):
        return rows_at(total, bit * HALF_Q, HALF_Q), rows_at(
            total, (1 - bit) * HALF_Q, HALF_Q
        )

    def weight(left, right, col, occupied_energy, virtual_energy, virtual_count):
        row = px * QUARTER + bit * HALF_Q
        rows = row + jnp.arange(HALF_Q, dtype=jnp.int32)
        cols = col + jnp.arange(COLS, dtype=jnp.int32)
        energy_rows = lax.dynamic_slice_in_dim(virtual_energy, row, HALF_Q)
        energy_cols = lax.dynamic_slice_in_dim(virtual_energy, col, COLS)
        keep_rows = (rows < virtual_count[left]).astype(jnp.float32)
        keep_cols = (cols < virtual_count[right]).astype(jnp.float32)
        denominator = (
            energy_rows[:, None]
            + energy_cols[None, :]
            - occupied_energy[left]
            - occupied_energy[right]
        )
        return keep_rows[:, None] * keep_cols[None, :] / denominator

    def join(part, other):
        return jnp.where(
            bit == 0,
            jnp.concatenate([part, other], 0),
            jnp.concatenate([other, part], 0),
        )

    def in_order(pieces):
        whole = jnp.zeros((X * QUARTER, pieces[0].shape[1]), jnp.float32)
        for r, piece in enumerate(pieces):
            whole = lax.dynamic_update_slice_in_dim(
                whole, piece, (px - r) % X * QUARTER, 0
            )
        return whole

    one, two, three = base, base + 1, (base + 2) % ORB

    other = move(own, SWAP)
    slab_one = jnp.where(first, own, other)
    slab_two = jnp.where(first, other, own)
    near = move(rows_at(slab_one, core * ROWS, ROWS), DOWN)
    one_cols = cols_at(slab_one, at, COLS)
    two_cols = cols_at(slab_two, at, COLS)

    inner = pair_term(slab_one, slab_two, two_cols, one_cols)
    inner_sends = send_x(inner)
    inner_parts = around(inner_sends)
    energies = after((occupied_energy, virtual_energy, virtual_count), inner_sends)
    inner_weight = weight(one, two, at, *energies)
    outer_weight = weight(two, three, at, *energies)
    near_two = rows_at(slab_two, core * ROWS, ROWS)
    far_two = rows_at(slab_two, (1 - core) * ROWS, ROWS)
    near_two_cols, far_two_cols = cols_at(near_two, at, COLS), cols_at(far_two, at, COLS)
    prepared = (near_two, far_two, near_two_cols, far_two_cols)
    ready = after((inner_parts, inner_weight, outer_weight), prepared)
    inner_parts, inner_weight, outer_weight = ready
    inner_kept, inner_sent = halves(add_x(inner_parts))
    inner_next = move(inner_sent, ALONG[1])

    near = after(near, inner_sent)
    far = move(near, SWAP)
    near_cols = cols_at(near, at, COLS)
    outer_near = pair_term(near_two, near, near_cols, near_two_cols)
    far = after(far, outer_near)
    far_cols = cols_at(far, at, COLS)
    outer = outer_near + pair_term(far_two, far, far_cols, far_two_cols)

    left, right = slice(0, CHUNK), slice(CHUNK, COLS)
    sends = [send_x(outer[:, w]) for w in (left, right)]
    parts = [around(sends[n]) for n in (0, 1)]
    kept_a, sent_a = halves(add_x(after(parts[0], sends)))
    next_a = move(sent_a, ALONG[1])
    inner_kept = inner_kept + after(inner_next, sent_a)
    inner_far = move(inner_kept, ALONG[2])
    kept_a = kept_a + after(next_a, inner_kept)
    far_a = move(kept_a, ALONG[2])
    parts_b = after(parts[1], kept_a)
    sum_b = add_x(parts_b)
    kept_b, sent_b = halves(sum_b)
    next_b = move(sent_b, ALONG[1])

    inner_t = (inner_kept + after(inner_far, sent_b)) * inner_weight
    inner_other = move(inner_t, ALONG[1])
    t_a = (kept_a + after(far_a, inner_t)) * outer_weight[:, left]
    other_a = move(t_a, ALONG[1])
    kept_b = kept_b + after(next_b, t_a)
    far_b = move(kept_b, ALONG[2])

    quarter_a = join(t_a, after(other_a, kept_b))
    pieces_a = around([quarter_a] * X)
    inner_quarter = join(inner_t, after(inner_other, quarter_a))
    inner_next = move(inner_quarter, ACROSS[1])
    t_b = (kept_b + after(far_b, inner_quarter)) * outer_weight[:, right]
    other_b = move(t_b, ALONG[1])

    all_a = in_order(after(pieces_a, t_b))
    leaving_a = dot(slab_two, all_a, 1, 0)
    incoming_a = [move(leaving_a, UP[c]) for c in (0, 1)]
    quarter_b = join(t_b, after(other_b, leaving_a))
    pieces_b = around([quarter_b] * X)
    inner_pair = jnp.concatenate([inner_quarter, after(inner_next, quarter_b)], 0)
    inner_rest = move(inner_pair, ACROSS[3])
    all_b = in_order(after(pieces_b, inner_pair))
    outgoing = dot(slab_two, all_b, 1, 0)
    incoming_b = [move(outgoing, UP[c]) for c in (0, 1)]
    incoming = [incoming_a[0], incoming_b[0], incoming_a[1], incoming_b[1]]

    inner_all = jnp.zeros((X * QUARTER, COLS), jnp.float32)
    inner_rest = after(inner_rest, outgoing)
    for q, d in ((inner_pair, 0), (inner_rest, 3)):
        for part, e in ((q[:QUARTER], d), (q[QUARTER:], d ^ 1)):
            inner_all = lax.dynamic_update_slice_in_dim(
                inner_all, part, (px ^ e) * QUARTER, 0
            )
    to_one = dot(two_cols, inner_all, 1, 1)
    to_two = dot(slab_one, inner_all, 1, 0)
    three_cols = jnp.where(
        first,
        jnp.concatenate([near_cols, far_cols], 0),
        jnp.concatenate([far_cols, near_cols], 0),
    )
    three_cols, all_a, all_b = after((three_cols, all_a, all_b), outgoing)
    beyond = dot(three_cols[:, left], all_a, 1, 1) + dot(three_cols[:, right], all_b, 1, 1)
    blank = jnp.zeros_like(to_two)
    to_two = beyond + jnp.where(
        first,
        jnp.concatenate([to_two, blank], 1),
        jnp.concatenate([blank, to_two], 1),
    )
    crossed = move(jnp.where(first, to_two, to_one), SWAP)
    crossed, incoming = after((crossed, incoming))
    density = jnp.where(first, to_one, to_two) + crossed + jnp.concatenate(incoming, 1)
    return density[None]


def solution(mesh):
    placed = (P("orb", "aux", None), P(), P(), P())
    return jax.shard_map(
        shards, mesh=mesh, in_specs=placed, out_specs=P("orb", "aux", None), check_vma=False
    )
```
